32 devices in a mesh: seq: 8 (over z, x), hid: 4 (over y, core).
Axes of the slice: x: 2, y: 2, z: 4, core: 2. Of those that a mesh axis runs over, the one named last changes fastest.
Arguments:
- tokens: bfloat16 [1024, 4096], P('seq', 'hid'), may hold values from -6 to 6
- hidden_grad: bfloat16 [1024, 14336], P('seq', 'hid'), may hold values from -6 to 6
- gate_blocks: bfloat16 [4, 448, 128, 128], P('hid', 'seq'), may hold values from -0.125 to 0.125
- up_blocks: bfloat16 [4, 448, 128, 128], P('hid', 'seq'), may hold values from -0.125 to 0.125
- gate_rows: int32 [4, 448], P('hid'), may hold values from 0 to 31, as said below
- gate_cols: int32 [4, 448], P('hid'), may hold values from 0 to 27
- gate_count: int32 [4], P('hid'), may hold values from 56 to 448, as said below
- up_rows: int32 [4, 448], P('hid'), may hold values from 0 to 31, as said below
- up_cols: int32 [4, 448], P('hid'), may hold values from 0 to 27
- up_count: int32 [4], P('hid'), may hold values from 56 to 448, as said below
Outputs:
- hidden: bfloat16 [1024, 14336], P('seq', 'hid')
- input_grad: bfloat16 [1024, 4096], P('seq', 'hid')
- gate_block_grads: bfloat16 [4, 448, 128, 128], P('hid', 'seq')
- up_block_grads: bfloat16 [4, 448, 128, 128], P('hid', 'seq')
The draws below stay inside these ranges and needn't reach their ends.
Inputs may be any that keep to these rules, and one draw needn't show every extreme that they name: For each panel, the pairs (gate_rows, gate_cols) over all 448 slots are distinct. `gate_count`: slots at or after a panel's count hold no block of the matrix. For each panel, the pairs (up_rows, up_cols) over all 448 slots are distinct. `up_count`: slots at or after a panel's count hold no block of the matrix.
All inputs are finite; a program needn't handle non-finite values.
Results may differ from the reference program's by a relative error of at most 0.018.
Values may be sent and summed in bfloat16 or wider, within the bound.
A program may use at most 192 MiB of HBM per device.

```python
import math
import jax
import jax.numpy as jnp
from jax import lax

D = 4096
FF = 14336
BS = 128
TOK_DEV = 128
TOKENS = 1024
CAP = 448
N_SEQ = 8
N_HID = 4


def slot_positions(key, salt):
    total_blocks = D // BS * (FF // N_HID // BS)
    panel_keys = jax.random.split(jax.random.fold_in(key, salt), N_HID)

    def one_panel(panel_key):
        return jax.random.permutation(panel_key, total_blocks)[:CAP]
    return jax.vmap(one_panel)(panel_keys).astype(jnp.int32)


def slot_counts(key, salt):
    lowest = CAP // 8
    highest = CAP // 2
    first, second = jax.random.split(jax.random.fold_in(key, salt), 2)
    counts = jax.random.randint(first, (N_HID,), lowest, highest + 1)
    order = jax.random.permutation(second, N_HID)
    counts = jnp.where(order == 0, CAP, counts)
    counts = jnp.where(order == 1, lowest, counts)
    return counts.astype(jnp.int32)


def draw_gate_rows(key, part):
    return (slot_positions(key, 11) // (FF // N_HID // BS)).astype(jnp.int32)


def draw_gate_cols(key, part):
    return (slot_positions(key, 11) % (FF // N_HID // BS)).astype(jnp.int32)


def draw_up_rows(key, part):
    return (slot_positions(key, 12) // (FF // N_HID // BS)).astype(jnp.int32)


def draw_up_cols(key, part):
    return (slot_positions(key, 12) % (FF // N_HID // BS)).astype(jnp.int32)


def draw_gate_count(key, part):
    return slot_counts(key, 21)


def draw_up_count(key, part):
    return slot_counts(key, 22)


def levels(own_key, dims, cuts, low, high):
    loudness, own = 1.0, jax.random.fold_in(own_key, 6)
    for dim, shards_of in cuts:
        heights = jnp.exp(jax.random.uniform(jax.random.fold_in(own, dim), (shards_of,), jnp.float32, low / len(cuts), high / len(cuts)))
        loudness = loudness * jnp.repeat(heights, dims[dim] // shards_of).reshape([-1 if axis == dim else 1 for axis in range(len(dims))])
    return loudness


def centred(own_key, shape, width, bound, cuts=(), dtype=jnp.bfloat16):
    entries = jax.random.normal(own_key, shape, jnp.float32) * width
    if len(cuts) > 0:
        entries = levels(own_key, shape, cuts, -0.22, 0.18) * entries
    return jnp.clip(entries, min=-bound, max=bound).astype(dtype)


def setup_inputs(seed: int = 0) -> dict:
    keys = jax.random.split(jax.random.key(seed), 11)
    return {
        "tokens": centred(keys[0], (TOKENS, D), 1.0, 6.0, ((0, 8), (1, 4))),
        "hidden_grad": centred(keys[1], (TOKENS, FF), 1.0, 6.0, ((0, 8), (1, 4))),
        "gate_blocks": centred(keys[2], (N_HID, CAP, BS, BS), (D // 2) ** -0.5, 0.125, ((0, 4), (1, 8))),
        "up_blocks": centred(keys[3], (N_HID, CAP, BS, BS), (D // 2) ** -0.5, 0.125, ((0, 4), (1, 8))),
        "gate_rows": draw_gate_rows(jax.random.fold_in(keys[10], 71), 0),
        "gate_cols": draw_gate_cols(jax.random.fold_in(keys[10], 71), 0),
        "gate_count": draw_gate_count(jax.random.fold_in(keys[10], 71), 0),
        "up_rows": draw_up_rows(jax.random.fold_in(keys[10], 71), 0),
        "up_cols": draw_up_cols(jax.random.fold_in(keys[10], 71), 0),
        "up_count": draw_up_count(jax.random.fold_in(keys[10], 71), 0),
    }


def placement_table(indices, active, extent):
    return (indices[:, None] == jnp.arange(extent)[None, :]).astype(jnp.float32) * active[:, None]

def reference(tokens, hidden_grad, gate_blocks, up_blocks, gate_rows, gate_cols, gate_count, up_rows, up_cols, up_count):
    row_blocks = D // BS
    panel_width = FF // N_HID
    col_blocks = panel_width // BS
    slot_ids = jnp.arange(CAP)
    scale = 1.0 / math.sqrt(TOKENS)
    highest = lax.Precision.HIGHEST
    token_tiles = tokens.reshape(N_SEQ, TOK_DEV, row_blocks, BS)
    input_total = jnp.zeros((N_SEQ, TOK_DEV, row_blocks, BS), jnp.float32)
    hidden_parts = []
    gate_grads = []
    up_grads = []
    for panel_index in range(N_HID):
        matrices = []
        for blocks, rows, columns, counts in ((gate_blocks, gate_rows, gate_cols, gate_count), (up_blocks, up_rows, up_cols, up_count)):
            active = (slot_ids < counts[panel_index]).astype(jnp.float32)
            matrices.append((blocks[panel_index].astype(jnp.float32), rows[panel_index], columns[panel_index], active, placement_table(columns[panel_index], active, col_blocks), placement_table(rows[panel_index], active, row_blocks)))
        upstream_all = hidden_grad[:, panel_index * panel_width:(panel_index + 1) * panel_width].reshape(N_SEQ, TOK_DEV, col_blocks, BS)

        def group_step(carry, inputs):
            tiles, upstream = inputs
            picked_inputs = []
            preacts = []
            for weights, rows, columns, active, col_table, row_table in matrices:
                picked = jnp.take(tiles, rows, axis=1).astype(jnp.float32)
                products = jnp.einsum('tsk,skn->tsn', picked, weights, precision=highest)
                preacts.append(jnp.einsum('tsn,sc->tcn', products, col_table, precision=highest))
                picked_inputs.append(picked)
            sigma = jax.nn.sigmoid(preacts[0])
            activated = preacts[0] * sigma
            slope = sigma * (1.0 + preacts[0] * (1.0 - sigma))
            hidden_here = (activated * preacts[1]).astype(jnp.bfloat16)
            upstream_wide = upstream.astype(jnp.float32)
            grads = ((upstream_wide * preacts[1] * slope).astype(jnp.bfloat16), (upstream_wide * activated).astype(jnp.bfloat16))
            input_part = jnp.zeros((TOK_DEV, row_blocks, BS), jnp.float32)
            new_carry = []
            for which in range(2):
                weights, rows, columns, active, col_table, row_table = matrices[which]
                picked_grad = jnp.take(grads[which], columns, axis=1).astype(jnp.float32)
                returned = jnp.einsum('tsn,skn->tsk', picked_grad, weights, precision=highest)
                input_part = input_part + jnp.einsum('tsk,sr->trk', returned, row_table, precision=highest)
                block_term = jnp.einsum('tsk,tsn->skn', picked_inputs[which], picked_grad, precision=highest) * active[:, None, None]
                rounded = lax.optimization_barrier(block_term.astype(jnp.bfloat16)).astype(jnp.float32)
                new_carry.append(carry[which] + rounded)
            return ((new_carry[0], new_carry[1]), (hidden_here, input_part.astype(jnp.bfloat16)))
        start_carry = (jnp.zeros((CAP, BS, BS), jnp.float32), jnp.zeros((CAP, BS, BS), jnp.float32))
        sums, outputs = lax.scan(group_step, start_carry, (token_tiles, upstream_all))
        hidden_parts.append(outputs[0].reshape(TOKENS, panel_width))
        input_total = input_total + outputs[1].astype(jnp.float32)
        gate_grads.append((sums[0] * scale).astype(jnp.bfloat16))
        up_grads.append((sums[1] * scale).astype(jnp.bfloat16))
    hidden = jnp.concatenate(hidden_parts, axis=1)
    input_grad = input_total.reshape(TOKENS, D).astype(jnp.bfloat16)
    return (hidden, input_grad, jnp.stack(gate_grads), jnp.stack(up_grads))
```

```python
import functools
import math

import jax
import jax.numpy as jnp
from jax import lax
from jax.experimental import pallas as pl
from jax.experimental.pallas import tpu as pltpu
from jax.sharding import Mesh, PartitionSpec as P

F32 = jnp.float32
BF16 = jnp.bfloat16
VMEM = pltpu.VMEM
SMEM = pltpu.SMEM
LIMIT = 66000000


def lanes(index, block):
    return pl.ds(pl.multiple_of(index * block, block), block)


def each_group(live, unroll, body):
    lax.fori_loop(0, (live + unroll - 1) // unroll, lambda i, c: (body(i * unroll), c)[1], 0)


def forward_kernel(own, block, per, unroll, base_ref, live_ref, rows_ref, cols_ref, tok_ref, mine_ref, other_ref, out_ref, acc):
    zc, tok_rows = tok_ref.shape[0], tok_ref.shape[2]
    spare = acc.shape[-1] // block - 1
    acc[...] = jnp.zeros_like(acc)
    for half, w_ref in enumerate((mine_ref, other_ref)):
        base = base_ref[half]
        live = jnp.clip(live_ref[0] - base, 0, own)

        def body(start, base=base, w_ref=w_ref, live=live):
            parts = []
            for u in range(unroll):
                row = rows_ref[0, base + start + u]
                x = tok_ref[:, row // per, :, lanes(row % per, block)]
                prod = jnp.dot(x.reshape(zc * tok_rows, block), w_ref[start + u], preferred_element_type=F32)
                parts.append(prod)
            for u, prod in enumerate(parts):
                col = jnp.where(start + u < live, cols_ref[0, base + start + u], spare)
                acc[:, lanes(col, block)] += prod

        each_group(live, unroll, body)
    for z in range(zc):
        out_ref[z] = acc[z * tok_rows : (z + 1) * tok_rows, : spare * block].astype(BF16)


def input_kernel(own, block, unroll, first, base_ref, live_ref, rows_ref, cols_ref, grad_ref, mine_ref, other_ref, *rest):
    prev_ref = None if first else rest[0]
    out_ref, acc = rest[-2:]
    zc, tok_rows = grad_ref.shape[0], grad_ref.shape[1]
    hs, width = out_ref.shape[0], out_ref.shape[3]
    spare = acc.shape[-1] // block - 1
    if first:
        acc[...] = jnp.zeros_like(acc)
    else:
        for h in range(hs):
            for z in range(zc):
                acc[z * tok_rows : (z + 1) * tok_rows, h * width : (h + 1) * width] = prev_ref[h, z]
    for half, w_ref in enumerate((mine_ref, other_ref)):
        base = base_ref[half]
        live = jnp.clip(live_ref[0] - base, 0, own)

        def body(start, base=base, w_ref=w_ref, live=live):
            parts = []
            for u in range(unroll):
                x = grad_ref[:, :, lanes(cols_ref[0, base + start + u], block)].reshape(zc * tok_rows, block)
                prod = lax.dot_general(x, w_ref[start + u], (((1,), (1,)), ((), ())), preferred_element_type=F32)
                parts.append(prod)
            for u, prod in enumerate(parts):
                row = jnp.where(start + u < live, rows_ref[0, base + start + u], spare)
                acc[:, lanes(row, block)] += prod

        each_group(live, unroll, body)
    for h in range(hs):
        for z in range(zc):
            piece = acc[z * tok_rows : (z + 1) * tok_rows, h * width : (h + 1) * width]
            out_ref[h, z] = piece.astype(out_ref.dtype)


def flip_kernel(block, per, tok_ref, out_ref):
    zc, hs, tok_rows = tok_ref.shape[0], tok_ref.shape[1], tok_ref.shape[2]

    def flip(row, carry):
        x = tok_ref[:, row // per, :, lanes(row % per, block)]
        out_ref[0, row] = x.reshape(zc * tok_rows, block).T
        return carry

    lax.fori_loop(0, hs * per, flip, 0)


def weight_kernel(own, block, unroll, steps, half, base_ref, live_ref, rows_ref, cols_ref, flip_ref, grad_ref, out_ref, acc):
    zc, tok_rows = grad_ref.shape[0], grad_ref.shape[1]
    base = base_ref[half]
    live = jnp.clip(live_ref[0] - base, 0, own)
    step = pl.program_id(0)

    def body(start):
        for u in range(unroll):
            row = rows_ref[0, base + start + u]
            col = cols_ref[0, base + start + u]
            g = grad_ref[:, :, lanes(col, block)].reshape(zc * tok_rows, block)
            prod = jnp.dot(flip_ref[0, row], g, preferred_element_type=F32)
            value = jnp.where(start + u < live, prod, 0.0)
            if steps == 1:
                out_ref[start + u] = value.astype(BF16)
            else:
                acc[start + u] = value + jnp.where(step == 0, 0.0, acc[start + u])

    def blank(slot, carry):
        if steps == 1:
            out_ref[slot] = jnp.zeros((block, block), BF16)
        else:
            acc[slot] = jnp.zeros((block, block), F32)
        return carry

    each_group(live, unroll, body)
    lax.fori_loop(live, own, blank, 0)
    if steps > 1:

        @pl.when(step == steps - 1)
        def _():
            out_ref[...] = acc[...].astype(BF16)


def on_device(
    zs, xs, hs, tokens, hidden_grad, gate_blocks, up_blocks, gate_rows, gate_cols, gate_count, up_rows, up_cols, up_count
):
    tok_rows, feat = tokens.shape
    width = hidden_grad.shape[1]
    own, block = gate_blocks.shape[1], gate_blocks.shape[2]
    per = feat // block
    unroll = math.gcd(own, 4)
    zc = math.gcd(zs, 4)
    steps = zs // zc
    many = zc * tok_rows
    zpos = lax.axis_index("z")
    xpos = lax.axis_index("x")
    flip_x = [(s, s ^ 1) for s in range(xs)]
    base = jnp.stack([(zpos * xs + xpos) * own, (zpos * xs + (xpos ^ 1)) * own]).astype(jnp.int32)
    gate_lists = (base, gate_count, gate_rows, gate_cols)
    up_lists = (base, up_count, up_rows, up_cols)
    smem = [pl.BlockSpec(memory_space=SMEM)] * 4
    block_spec = pl.BlockSpec((own, block, block), lambda i: (0, 0, 0))
    tok_spec = pl.BlockSpec((zc, hs, tok_rows, feat), lambda i: (i, 0, 0, 0))
    back_spec = pl.BlockSpec((hs, zc, tok_rows, feat), lambda i: (0, i, 0, 0))
    grad_spec = pl.BlockSpec((zc, tok_rows, width), lambda i: (i, 0, 0))
    flip_spec = pl.BlockSpec((1, hs * per, block, many), lambda i: (i, 0, 0, 0))
    params = pltpu.CompilerParams(vmem_limit_bytes=LIMIT)
    cost = pl.CostEstimate(flops=8 * zs * tok_rows * 2 * own * block * block, bytes_accessed=2**23, transcendentals=0)

    gate_mine, up_mine = gate_blocks[0], up_blocks[0]
    gate_other = lax.ppermute(gate_mine, "x", flip_x)
    up_other = lax.ppermute(up_mine, "x", flip_x)
    tok_all = lax.all_gather(tokens, ("z", "hid")).reshape(zs, hs, tok_rows, feat)

    def project(lists, mine, other):
        return pl.pallas_call(
            functools.partial(forward_kernel, own, block, per, unroll),
            grid=(steps,),
            in_specs=smem + [tok_spec, block_spec, block_spec],
            out_specs=grad_spec,
            out_shape=jax.ShapeDtypeStruct((zs, tok_rows, width), BF16),
            scratch_shapes=[VMEM((many, width + block), F32)],
            compiler_params=params,
            cost_estimate=cost,
        )(*lists, tok_all, mine, other)

    def bring_back(lists, grads, mine, other, prev):
        first = prev is None
        return pl.pallas_call(
            functools.partial(input_kernel, own, block, unroll, first),
            grid=(steps,),
            in_specs=smem + [grad_spec, block_spec, block_spec] + ([] if first else [back_spec]),
            out_specs=back_spec,
            out_shape=jax.ShapeDtypeStruct((hs, zs, tok_rows, feat), F32 if first else BF16),
            scratch_shapes=[VMEM((many, hs * feat + block), F32)],
            compiler_params=params,
            cost_estimate=cost,
        )(*lists, grads, mine, other, *(() if first else (prev,)))

    def weight_terms(lists, flipped, grads, half):
        return pl.pallas_call(
            functools.partial(weight_kernel, own, block, unroll, steps, half),
            grid=(steps,),
            in_specs=smem + [flip_spec, grad_spec],
            out_specs=block_spec,
            out_shape=jax.ShapeDtypeStruct((own, block, block), BF16),
            scratch_shapes=[VMEM((own if steps > 1 else 1, block, block), F32)],
            compiler_params=params,
            cost_estimate=cost,
        )(*lists, flipped, grads)

    gate_part = project(gate_lists, gate_mine, gate_other)
    up_part = project(up_lists, up_mine, up_other)
    later, _ = lax.optimization_barrier((tok_all, up_part))
    flipped = pl.pallas_call(
        functools.partial(flip_kernel, block, per),
        grid=(steps,),
        in_specs=[tok_spec],
        out_specs=flip_spec,
        out_shape=jax.ShapeDtypeStruct((steps, hs * per, block, many), BF16),
        compiler_params=params,
        cost_estimate=cost,
        name="flip",
    )(later)
    gate_pre = lax.psum_scatter(gate_part, "z", scatter_dimension=0, tiled=False).astype(F32)
    up_pre = lax.psum_scatter(up_part, "z", scatter_dimension=0, tiled=False).astype(F32)
    gate_pre, flipped = lax.optimization_barrier((gate_pre, flipped))
    sigma = jax.nn.sigmoid(gate_pre)
    activated = gate_pre * sigma
    slope = sigma * (1.0 + gate_pre * (1.0 - sigma))
    hidden = (activated * up_pre).astype(BF16)
    upstream = hidden_grad.astype(F32)
    gate_grad = lax.all_gather((upstream * up_pre * slope).astype(BF16), "z")
    up_grad = lax.all_gather((upstream * activated).astype(BF16), "z")

    back = bring_back(gate_lists, gate_grad, gate_mine, gate_other, None)
    gate_terms = weight_terms(gate_lists, flipped, gate_grad, 1)
    gate_kept = weight_terms(gate_lists, flipped, gate_grad, 0)
    back, gate_terms, gate_kept = lax.optimization_barrier((back, gate_terms, gate_kept))
    gate_sent = lax.ppermute(gate_terms, "x", flip_x)
    back = bring_back(up_lists, up_grad, up_mine, up_other, back)
    back = lax.psum_scatter(back, "hid", scatter_dimension=0, tiled=False)
    input_grad = lax.psum_scatter(back, "z", scatter_dimension=0, tiled=False)
    up_sent = lax.ppermute(weight_terms(up_lists, flipped, up_grad, 1), "x", flip_x)
    up_kept = weight_terms(up_lists, flipped, up_grad, 0)
    scale = 1.0 / math.sqrt(tok_rows * zs * xs)
    gate_out = ((gate_kept.astype(F32) + gate_sent.astype(F32)) * scale).astype(BF16)
    up_out = ((up_kept.astype(F32) + up_sent.astype(F32)) * scale).astype(BF16)
    return hidden, input_grad, gate_out[None], up_out[None]


def solution(mesh):
    seq, hid = mesh.shape["seq"], mesh.shape["hid"]
    xs = 2
    zs = seq // xs
    inner = Mesh(mesh.devices.reshape(zs, xs, hid), ("z", "x", "hid"))
    zx = ("z", "x")
    placed = (
        P(zx, "hid"),
        P(zx, "hid"),
        P("hid", zx, None, None),
        P("hid", zx, None, None),
        P("hid", None),
        P("hid", None),
        P("hid"),
        P("hid", None),
        P("hid", None),
        P("hid"),
    )
    return jax.shard_map(
        functools.partial(on_device, zs, xs, hid),
        mesh=inner,
        in_specs=placed,
        out_specs=(P(zx, "hid"), P(zx, "hid"), P("hid", zx, None, None), P("hid", zx, None, None)),
        check_vma=False,
    )
```
